256 devices in a mesh: ctx: 8 (over z_lo, core), dp: 8 (over z_hi, y), head: 4 (over x).
Axes of the slice: x: 4, y: 4, z: 8 (z_hi: 2, z_lo: 4; z = z_hi * 4 + z_lo), core: 2. Of those that a mesh axis runs over, the one named last changes fastest.
Arguments:
- queries: bfloat16 [32768, 8, 128], P(('dp', 'ctx'), 'head'), parts along dimension 0, may hold values from -40 to 40
- keys: bfloat16 [32768, 128], P(('dp', 'ctx')), parts along dimension 0, may hold values from -6 to 6
- values: bfloat16 [32768, 128], P(('dp', 'ctx')), parts along dimension 0, may hold values from -6 to 6
- output: bfloat16 [32768, 8, 128], P(('dp', 'ctx'), 'head'), parts along dimension 0, may hold values from -6 to 6
- output_grad: bfloat16 [32768, 8, 128], P(('dp', 'ctx'), 'head'), parts along dimension 0, may hold values from -6 to 6
- block_doc: int32 [256], P('dp'), parts along dimension 0, may hold values from 0 to 3, never falling along the last dimension, each value on 1 to 24 neighbouring positions
Outputs:
- query_grad: bfloat16 [32768, 8, 128], P(('dp', 'ctx'), 'head'), parts along dimension 0
- key_grad: bfloat16 [32768, 128], P(('dp', 'ctx', 'head')), parts along dimension 0
- value_grad: bfloat16 [32768, 128], P(('dp', 'ctx', 'head')), parts along dimension 0
The draws below stay inside these ranges and needn't reach their ends.
There are 8 independent parts, one for each index of `dp`. The reference program is written for one: setup_inputs(seed, part) draws one part's arguments, and reference() takes and returns one part's arrays. A program takes and returns all parts, laid end to end along the dimension named above; each array names one. Nothing has to cross between parts.
Inputs may be any that keep to these rules, and one draw needn't show every extreme that they name: block_doc[b] is the document of tokens b * 128 to (b + 1) * 128 - 1; ids never fall; each of the 4 documents spans 1 to 24 blocks, and one spans exactly 24.
All inputs are finite; a program needn't handle non-finite values.
Results may differ from the reference program's by a relative error of at most 0.0049.
Values may be sent and summed in bfloat16 or wider, within the bound.
No kernel may reach another device: no remote copies, remote signals or barrier semaphores. Data moves between devices by JAX's collectives and lax.ppermute only.
A program may use at most 64 MiB of HBM per device.

```python
import math
import jax
import jax.numpy as jnp
import numpy as np
from jax import lax

HEADS = 8
HD = 128
TOK_DEV = 512
BLK = 128
DOCS = 4
TOKENS = 4096
NB = 32
DOC_MOST = 24
N_CTX = 8


def pair_draw(key):
    seeded = jax.random.fold_in(key, 7331)
    key_query, key_key = jax.random.split(seeded)
    query_out = jax.random.truncated_normal(key_query, -6.0, 6.0, (TOKENS, HEADS, HD), jnp.float32)
    key_out = jax.random.truncated_normal(key_key, -6.0, 6.0, (TOKENS, HD), jnp.float32)
    return (query_out, key_out)


def draw_queries(key, part):
    return pair_draw(key)[0].astype(jnp.bfloat16)


def draw_keys(key, part):
    return pair_draw(key)[1].astype(jnp.bfloat16)


def block_levels(key, extent, pieces, smallest, largest):
    level = 1.0
    for position, parts in pieces:
        steps = jax.random.uniform(jax.random.fold_in(jax.random.fold_in(key, 6), position), (parts,), jnp.float32, smallest / len(pieces), largest / len(pieces))
        level = level * jnp.repeat(jnp.exp(steps), extent[position] // parts).reshape((-1,) + (1,) * (len(extent) - 1 - position))
    return level


def profile(amount, total, reach, slope):
    weights = [(1 << 20) // math.isqrt(grade ** slope) + 1 for grade in range(2, amount + 1)]
    spare, given = total - reach - (amount - 1), [1] * (amount - 1)
    while spare > 0:
        candidates = [i for i in range(amount - 1) if given[i] < reach]
        pool, budget = sum([weights[i] for i in candidates]), spare
        for i in candidates:
            addition = min(reach - given[i], max(1, budget * weights[i] // pool), spare)
            given[i] = given[i] + addition
            spare = spare - addition
    return np.array([reach] + given)


def uneven_parts(stream_key, count, total, bound, slope):
    if count == 2:
        one = jax.random.randint(stream_key, (), max(1, total - bound), min(bound, total - 1) + 1)
        return jnp.stack([one, total - one])
    tallies = jnp.asarray(profile(count, total, bound, slope), jnp.int32)
    twos = (count - 1) // 2
    donor, taker = tallies[1:1 + 2 * twos:2], tallies[2:2 + 2 * twos:2]
    margin = jnp.minimum(donor - 1, bound - taker)
    shifted = jax.random.randint(jax.random.fold_in(stream_key, 1), (twos,), 0, 1 << 20) % (margin + 1)
    tallies = tallies.at[1:1 + 2 * twos:2].set(donor - shifted).at[2:2 + 2 * twos:2].set(taker + shifted)
    return tallies[jax.random.permutation(jax.random.fold_in(stream_key, 2), count)]


def centred(key, extent, scale, bound, cuts=(), kind=jnp.bfloat16):
    level = block_levels(key, extent, cuts, -0.22, 0.18) if cuts else 1.0
    drawn = jax.random.normal(key, extent, jnp.float32) * scale * level
    return jnp.minimum(jnp.maximum(drawn, -bound), bound).astype(kind)


def setup_inputs(seed: int = 0, part: int = 0) -> dict:
    arg_keys = jax.random.split(jax.random.key(seed), 7)
    own_keys = jax.random.split(jax.random.fold_in(arg_keys[6], part), 7)
    return {
        "queries": draw_queries(jax.random.fold_in(jax.random.fold_in(arg_keys[6], part), 71), part),
        "keys": draw_keys(jax.random.fold_in(jax.random.fold_in(arg_keys[6], part), 71), part),
        "values": centred(own_keys[2], (TOKENS, HD), 1.0, 6.0, ((0, 8),)),
        "output": centred(own_keys[3], (TOKENS, HEADS, HD), 1.0, 6.0, ((0, 8), (1, 4))),
        "output_grad": centred(own_keys[4], (TOKENS, HEADS, HD), 1.0, 6.0, ((0, 8), (1, 4))),
        "block_doc": jnp.searchsorted(jnp.cumsum(uneven_parts(own_keys[5], DOCS, NB, DOC_MOST, 0)), jnp.arange(NB), side="right").astype(jnp.int32),
    }


masked_score = -1.0e30


def reference(queries, keys, values, output, output_grad, block_doc):
    inv_root = HD ** -0.5
    doc_tok = jnp.repeat(block_doc, BLK)
    positions = jnp.arange(TOKENS, dtype=jnp.int32)
    key_float = keys.astype(jnp.float32)
    value_float = values.astype(jnp.float32)
    row_delta = jnp.sum(output_grad.astype(jnp.float32) * output.astype(jnp.float32), axis=-1)

    def query_block(carried, block_index):
        key_acc, value_acc = carried
        first_row = (block_index * TOK_DEV).astype(jnp.int32)
        query_tile = lax.dynamic_slice_in_dim(queries, first_row, TOK_DEV, 0).astype(jnp.float32)
        grad_tile = lax.dynamic_slice_in_dim(output_grad, first_row, TOK_DEV, 0).astype(jnp.float32)
        delta_tile = lax.dynamic_slice_in_dim(row_delta, first_row, TOK_DEV, 0)
        query_pos = lax.dynamic_slice_in_dim(positions, first_row, TOK_DEV, 0)
        query_doc = lax.dynamic_slice_in_dim(doc_tok, first_row, TOK_DEV, 0)
        visible_mask = (positions[None, :] <= query_pos[:, None]) & (doc_tok[None, :] == query_doc[:, None])
        score_tile = jnp.einsum("bhd,kd->bhk", query_tile, key_float) * inv_root
        score_tile = jnp.where(visible_mask[:, None, :], score_tile, masked_score)
        running_max = jnp.max(score_tile, axis=-1)
        terms = jnp.where(visible_mask[:, None, :], jnp.exp(score_tile - running_max[..., None]), 0.0)
        log_total = running_max + jnp.log(jnp.sum(terms, axis=-1))
        prob = jnp.where(visible_mask[:, None, :], jnp.exp(score_tile - log_total[..., None]), 0.0)
        prob_low = prob.astype(jnp.bfloat16).astype(jnp.float32)
        prob_grad = jnp.einsum("bhd,kd->bhk", grad_tile, value_float)
        score_grad = (prob * (prob_grad - delta_tile[..., None])).astype(jnp.bfloat16).astype(jnp.float32)
        query_part = jnp.einsum("bhk,kd->bhd", score_grad, key_float) * inv_root
        key_acc = key_acc + jnp.einsum("bhk,bhd->kd", score_grad, query_tile) * inv_root
        value_acc = value_acc + jnp.einsum("bhk,bhd->kd", prob_low, grad_tile)
        return (key_acc, value_acc), query_part.astype(jnp.bfloat16)

    zero_grad = jnp.zeros((TOKENS, HD), jnp.float32)
    (key_acc, value_acc), query_parts = lax.scan(query_block, (zero_grad, zero_grad), jnp.arange(N_CTX, dtype=jnp.int32))
    query_grad = query_parts.reshape(TOKENS, HEADS, HD)
    return query_grad, key_acc.astype(jnp.bfloat16), value_acc.astype(jnp.bfloat16)
```

```python
import math

import jax
import jax.numpy as jnp
from jax import lax
from jax.experimental import pallas as pl
from jax.experimental.pallas import tpu as pltpu
from jax.sharding import PartitionSpec as P

BLK = 128
TILE = 256
floor_score = -1.0e30
masked_score = -2.0e30

NT = (((1,), (1,)), ((), ()))


def tile_bounds(ctx, starts, back, key_tile, key_rows, query_tile, shard_rows):
    key_base = (ctx - 2 * back) * shard_rows + key_tile * key_rows
    partner = ctx + 1 - 2 * lax.rem(ctx, 2)
    shard = jnp.where(query_tile < 2, ctx, partner)
    query_base = shard * shard_rows + lax.rem(query_tile, 2) * TILE
    block = lax.div(query_base, BLK)
    first, last = starts[block], starts[block + 1]
    seen = (key_base <= query_base + TILE - 1) & (key_base + key_rows - 1 >= first)
    inside = (key_base + key_rows - 1 <= query_base) & (key_base >= last)
    return (key_base, query_base, first, last), seen, inside


def tile_mask(edge, offset, rows, width):
    key_base, query_base, first, last = edge
    key_pos = key_base + offset + lax.broadcasted_iota(jnp.int32, (rows, width), 0)
    lane = lax.rem(lax.broadcasted_iota(jnp.int32, (1, width), 1), TILE)
    query_pos = query_base + lane
    start = jnp.where(lane < BLK, first, last)
    return (key_pos <= query_pos) & (key_pos >= start)


def each_tile(ctx, starts, back, shard_rows, tiles, visit):
    def step(query_tile, carry):
        _, seen, inside = tile_bounds(ctx, starts, back, 0, shard_rows, query_tile, shard_rows)

        @pl.when(inside)
        def _():
            visit(query_tile, 0, shard_rows, None)

        @pl.when(seen & jnp.logical_not(inside))
        def _():
            def part(key_tile, carry):
                edge, seen, _ = tile_bounds(ctx, starts, back, key_tile, TILE, query_tile, shard_rows)

                @pl.when(seen)
                def _():
                    visit(query_tile, pl.multiple_of(key_tile * TILE, TILE), TILE, edge)

                return carry

            lax.fori_loop(0, shard_rows // TILE, part, 0)

        return carry

    @pl.when(ctx >= 2 * back)
    def _():
        lax.fori_loop(0, tiles, step, 0)


def stat_chunk(scale, ctx, starts, back, rows, key_ref, tops, sums):
    tiles, width = rows.shape[1], rows.shape[2]
    sub = BLK

    def visit(query_tile, base, count, edge):
        old = tops[query_tile]
        new = old
        scores = []
        for offset in range(0, count, sub):
            key = key_ref[pl.ds(base + offset, sub), :]
            score = lax.dot_general(key, rows[0, query_tile], NT, preferred_element_type=jnp.float32) * scale
            if edge is not None:
                score = jnp.where(tile_mask(edge, offset, sub, width), score, masked_score)
            score = score.reshape(sub // 8, 8, width)
            new = jnp.maximum(new, jnp.max(score, axis=0))
            scores.append(score)
        total = sums[query_tile] * jnp.exp2(old - new)
        for score in scores:
            total = total + jnp.sum(jnp.exp2(score - new[None]), axis=0)
        sums[query_tile] = total
        tops[query_tile] = new

    each_tile(ctx, starts, back, key_ref.shape[0], tiles, visit)


def near_stats_body(scale, info, starts, rows, key_ref, tops, sums):
    tops[...] = jnp.full(tops.shape, floor_score, jnp.float32)
    sums[...] = jnp.zeros(sums.shape, jnp.float32)
    stat_chunk(scale, info[0], starts, 0, rows, key_ref, tops, sums)


def far_stats_body(scale, info, starts, rows, delta, tops_in, sums_in, *refs):
    keys, out, tops, sums = refs[:-3], refs[-3], refs[-2], refs[-1]
    tiles = rows.shape[1]
    tops[...] = tops_in[...]
    sums[...] = sums_in[...]
    for back, key_ref in enumerate(keys, 1):
        stat_chunk(scale, info[0], starts, back, rows, key_ref, tops, sums)
    for tile in range(tiles):
        top = jnp.max(tops[tile], axis=0, keepdims=True)
        out[tile : tile + 1, :] = top
        out[tiles + tile : tiles + tile + 1, :] = jnp.sum(
            sums[tile] * jnp.exp2(tops[tile] - top), axis=0, keepdims=True
        )
    half = tiles // 2
    out[2 * tiles : 2 * tiles + half, :] = delta[...]


def grad_body(scale, inv_root, backs, carried, info, starts, rows, mine, other, *refs):
    refs = list(refs)
    keys = [refs.pop(0) for _ in backs]
    if backs == (0,):
        own_value, pieces = refs.pop(0), None
    else:
        own_value, pieces = None, [refs.pop(0) for _ in range(4)]
    query_in = refs.pop(0) if carried else None
    kept, query_out, sends = refs[0], refs[1], refs[2:-5]
    logs, deltas, key_acc, value_acc, value_all = refs[-5:]
    owners = len(sends) + 1
    ctx, head = info[0], info[1]
    tiles, width = rows.shape[1], rows.shape[2]
    shard_rows, size = key_acc.shape
    half = tiles // 2
    query_out[...] = query_in[...] if carried else jnp.zeros(query_out.shape, jnp.float32)
    for tile in range(tiles):
        twin = (tile + half) % tiles
        top_a, top_b = mine[tile : tile + 1, :], other[twin : twin + 1, :]
        sum_a, sum_b = mine[tiles + tile : tiles + tile + 1, :], other[tiles + twin : tiles + twin + 1, :]
        top = jnp.maximum(top_a, top_b)
        total = sum_a * jnp.exp2(top_a - top) + sum_b * jnp.exp2(top_b - top)
        logs[tile] = top + jnp.log2(total)
        source = mine if tile < half else other
        at = 2 * tiles + tile % half
        deltas[tile] = source[at : at + 1, :]
    part = shard_rows // owners
    for slot, back in enumerate(backs):
        key_ref = keys[slot]
        if own_value is None:
            value_ref = value_all
            for turn in range(owners):
                at = pl.multiple_of(lax.rem(head + owners - turn, owners) * part, part)
                value_all[pl.ds(at, part), :] = pieces[turn][back - 1]
        else:
            value_ref = own_value
        key_acc[...] = jnp.zeros(key_acc.shape, jnp.float32)
        value_acc[...] = jnp.zeros(value_acc.shape, jnp.float32)

        def visit(query_tile, base, count, edge, key_ref=key_ref, value_ref=value_ref):
            query, grad = rows[0, query_tile], rows[1, query_tile]
            log_total, delta = logs[query_tile], deltas[query_tile]
            score_grads = []
            for offset in range(0, count, TILE):
                at = pl.ds(base + offset, TILE)
                key, value = key_ref[at, :], value_ref[at, :]
                score = lax.dot_general(key, query, NT, preferred_element_type=jnp.float32)
                prob_grad = lax.dot_general(value, grad, NT, preferred_element_type=jnp.float32)
                prob = jnp.exp2(score * scale - log_total)
                if edge is not None:
                    prob = jnp.where(tile_mask(edge, offset, TILE, width), prob, 0.0)
                score_grad = (prob * (prob_grad - delta)).astype(jnp.bfloat16)
                value_acc[at, :] += jnp.dot(prob.astype(jnp.bfloat16), grad, preferred_element_type=jnp.float32)
                key_acc[at, :] += jnp.dot(score_grad, query, preferred_element_type=jnp.float32)
                score_grads.append(score_grad)
            score_grad = jnp.concatenate(score_grads, axis=0)
            query_out[query_tile] += lax.dot_general(
                key_ref[pl.ds(base, count), :],
                score_grad,
                (((0,), (0,)), ((), ())),
                preferred_element_type=jnp.float32,
            )

        each_tile(ctx, starts, back, shard_rows, tiles, visit)

        for turn in range(owners):
            at = pl.ds(pl.multiple_of(lax.rem(head + turn, owners) * part, part), part)
            out = sends[turn - 1] if turn else kept
            out[slot, :, :size] = (key_acc[at, :] * inv_root).astype(out.dtype)
            out[slot, :, size:] = value_acc[at, :].astype(out.dtype)


def vmem(count):
    return [pl.BlockSpec(memory_space=pltpu.VMEM)] * count


def smem(count):
    return [pl.BlockSpec(memory_space=pltpu.SMEM)] * count


def limit(mib):
    return pltpu.CompilerParams(vmem_limit_bytes=mib << 20)


def local(queries, keys, values, output, output_grad, block_doc):
    shard_rows, heads, size = queries.shape
    cycle = lax.axis_size("ctx")
    owners = lax.axis_size("head")
    steps = cycle // 2
    ctx = lax.axis_index("ctx").astype(jnp.int32)
    head = lax.axis_index("head").astype(jnp.int32)
    inv_root = size ** (-0.5)
    scale = inv_root * math.log2(math.e)
    half = shard_rows // TILE
    tiles, width = 2 * half, heads * TILE
    part = shard_rows // owners
    twins = [(i, i ^ 1) for i in range(cycle)]

    def swap(array):
        return lax.ppermute(array, "ctx", twins)

    def shift(array, back):
        return lax.ppermute(array, "ctx", [(i, i + 2 * back) for i in range(cycle - 2 * back)])

    def unshift(array, back):
        return lax.ppermute(array, "ctx", [(i + 2 * back, i) for i in range(cycle - 2 * back)])

    def turned(array, turn):
        return lax.ppermute(array, "head", [(i, (i + turn) % owners) for i in range(owners)])

    value_part = lax.dynamic_slice_in_dim(values, head * part, part, 0)
    value_parts = jnp.stack([shift(value_part, back) for back in range(1, steps)])
    key_parts = [keys] + [shift(keys, back) for back in range(1, steps)]
    pieces = [value_parts] + [turned(value_parts, turn) for turn in range(1, owners)]

    def tiled(array):
        return array.reshape(half, TILE, heads, size).transpose(0, 2, 1, 3).reshape(half, width, size)

    own_rows = jnp.stack([tiled(queries), tiled(output_grad)])
    rows = jnp.concatenate([own_rows, swap(own_rows)], axis=1)
    delta = jnp.sum(output_grad.astype(jnp.float32) * output.astype(jnp.float32), axis=-1)
    delta = delta.reshape(half, TILE, heads).transpose(0, 2, 1).reshape(half, width)
    starts = BLK * jnp.sum((block_doc[None, :] < block_doc[:, None]).astype(jnp.int32), axis=1)
    info = jnp.stack([ctx, head])

    running = [jax.ShapeDtypeStruct((tiles, 8, width), jnp.float32)] * 2
    tops, sums = pl.pallas_call(
        lambda *refs: near_stats_body(scale, *refs),
        out_shape=tuple(running),
        in_specs=smem(2) + vmem(2),
        out_specs=tuple(vmem(2)),
        compiler_params=limit(12),
        name="near_stats",
    )(info, starts, rows, keys)
    stats = pl.pallas_call(
        lambda *refs: far_stats_body(scale, *refs),
        out_shape=jax.ShapeDtypeStruct((4 * tiles, width), jnp.float32),
        in_specs=smem(2) + vmem(3 + steps),
        out_specs=vmem(1)[0],
        scratch_shapes=[pltpu.VMEM((tiles, 8, width), jnp.float32)] * 2,
        compiler_params=limit(12),
        name="far_stats",
    )(info, starts, rows, delta, tops, sums, *key_parts[1:])
    other = swap(stats)

    def grads(backs, query_in):
        carried = query_in is not None
        count = len(backs)
        own = backs == (0,)
        ins = [key_parts[back] for back in backs] + ([values] if own else pieces) + ([query_in] if carried else [])
        return pl.pallas_call(
            lambda *refs: grad_body(scale, inv_root, backs, carried, *refs),
            out_shape=(
                jax.ShapeDtypeStruct((count, part, 2 * size), jnp.float32),
                jax.ShapeDtypeStruct((tiles, size, width), jnp.float32),
            )
            + (jax.ShapeDtypeStruct((count, part, 2 * size), jnp.bfloat16),) * (owners - 1),
            in_specs=smem(2) + vmem(3 + len(ins)),
            out_specs=tuple(vmem(1 + owners)),
            scratch_shapes=[pltpu.VMEM((tiles, 1, width), jnp.float32)] * 2
            + [pltpu.VMEM((shard_rows, size), jnp.float32)] * 2
            + [pltpu.VMEM((shard_rows, size), jnp.bfloat16)],
            input_output_aliases={4 + len(ins): 1} if carried else {},
            compiler_params=limit(16),
            name="grads_%d" % backs[0],
        )(info, starts, rows, stats, other, *ins)

    def mixed(kept, sends):
        total = kept
        for turn, sent in enumerate(sends, 1):
            total = total + turned(sent, turn).astype(jnp.float32)
        return total

    query_acc = None
    returned = []
    for backs in ((3, 2), (1,), (0,)):
        kept, query_acc, *sends = grads(backs, query_acc)
        total = mixed(kept, sends)
        for slot, back in enumerate(backs):
            if back:
                returned.append(unshift(total[slot].astype(jnp.bfloat16), back))
    total = total[0]
    for came in returned:
        total = total + came.astype(jnp.float32)
    total = total.astype(jnp.bfloat16)

    query_sum = query_acc[:half] + swap(query_acc[half:])
    query_grad = (query_sum * inv_root).reshape(half, size, heads, TILE).transpose(0, 3, 2, 1)
    query_grad = query_grad.reshape(shard_rows, heads, size).astype(jnp.bfloat16)
    return query_grad, total[:, :size], total[:, size:]


def solution(mesh):
    placed = (
        P(("dp", "ctx"), "head", None),
        P(("dp", "ctx"), None),
        P(("dp", "ctx"), None),
        P(("dp", "ctx"), "head", None),
        P(("dp", "ctx"), "head", None),
        P("dp"),
    )
    return jax.shard_map(
        local,
        mesh=mesh,
        in_specs=placed,
        out_specs=(
            P(("dp", "ctx"), "head", None),
            P(("dp", "ctx", "head"), None),
            P(("dp", "ctx", "head"), None),
        ),
        check_vma=False,
    )
```

```python
import math

import jax
import jax.numpy as jnp
from jax import lax
from jax.experimental import pallas as pl
from jax.experimental.pallas import tpu as pltpu
from jax.sharding import PartitionSpec as P


BLK = 128
TILE = 256
floor_score = -1.0e30
masked_score = -2.0e30

NT = (((1,), (1,)), ((), ()))


def tile_bounds(ctx, starts, back, key_tile, key_rows, query_tile, shard_rows):
    key_base = (ctx - 2 * back) * shard_rows + key_tile * key_rows
    partner = ctx + 1 - 2 * lax.rem(ctx, 2)
    shard = jnp.where(query_tile < 2, ctx, partner)
    query_base = shard * shard_rows + lax.rem(query_tile, 2) * TILE
    block = lax.div(query_base, BLK)
    first, last = starts[block], starts[block + 1]
    seen = (key_base <= query_base + TILE - 1) & (key_base + key_rows - 1 >= first)
    inside = (key_base + key_rows - 1 <= query_base) & (key_base >= last)
    return (key_base, query_base, first, last), seen, inside


def tile_mask(edge, offset, rows, width):
    key_base, query_base, first, last = edge
    key_pos = key_base + offset + lax.broadcasted_iota(jnp.int32, (rows, width), 0)
    lane = lax.rem(lax.broadcasted_iota(jnp.int32, (1, width), 1), TILE)
    query_pos = query_base + lane
    start = jnp.where(lane < BLK, first, last)
    return (key_pos <= query_pos) & (key_pos >= start)


def each_tile(ctx, starts, back, shard_rows, tiles, visit):
    def step(query_tile, carry):
        _, seen, inside = tile_bounds(ctx, starts, back, 0, shard_rows, query_tile, shard_rows)

        @pl.when(inside)
        def _():
            visit(query_tile, 0, shard_rows, None)

        @pl.when(seen & jnp.logical_not(inside))
        def _():
            def part(key_tile, carry):
                edge, seen, _ = tile_bounds(ctx, starts, back, key_tile, TILE, query_tile, shard_rows)

                @pl.when(seen)
                def _():
                    visit(query_tile, pl.multiple_of(key_tile * TILE, TILE), TILE, edge)

                return carry

            lax.fori_loop(0, shard_rows // TILE, part, 0)

        return carry

    @pl.when(ctx >= 2 * back)
    def _():
        lax.fori_loop(0, tiles, step, 0)


def stat_chunk(scale, ctx, starts, back, rows, key_ref, store, tops, sums):
    tiles, width = rows.shape[1], rows.shape[2]
    sub = 32

    def visit(query_tile, base, count, edge):
        top = tops[query_tile]
        total = sums[query_tile]
        scores = lax.dot_general(
            key_ref[pl.ds(base, count), :], rows[0, query_tile], NT, preferred_element_type=jnp.float32
        )
        for offset in range(0, count, sub):
            score = scores[offset : offset + sub] * scale
            if edge is not None:
                score = jnp.where(tile_mask(edge, offset, sub, width), score, masked_score)
            if store is not None:
                store[query_tile, pl.ds(base + offset, sub), :] = score
            score = score.reshape(sub // 8, 8, width)
            new = jnp.maximum(top, jnp.max(score, axis=0))
            total = total * jnp.exp2(top - new) + jnp.sum(jnp.exp2(score - new[None]), axis=0)
            top = new
        sums[query_tile] = total
        tops[query_tile] = top

    each_tile(ctx, starts, back, key_ref.shape[0], tiles, visit)


def near_stats_body(scale, info, starts, rows, key_ref, tops, sums):
    tops[...] = jnp.full(tops.shape, floor_score, jnp.float32)
    sums[...] = jnp.zeros(sums.shape, jnp.float32)
    stat_chunk(scale, info[0], starts, 0, rows, key_ref, None, tops, sums)


def far_stats_body(scale, backs, last, info, starts, rows, delta, tops_in, sums_in, *refs):
    count = len(backs)
    keys, store, outs = refs[:count], refs[count], refs[count + 1 :]
    tiles = rows.shape[1]
    tops, sums = outs[-2:]
    tops[...] = tops_in[...]
    sums[...] = sums_in[...]
    for slot, (back, key_ref) in enumerate(zip(backs, keys)):
        stat_chunk(scale, info[0], starts, back, rows, key_ref, store.at[slot], tops, sums)
    if last:
        out = outs[0]
        for tile in range(tiles):
            top = jnp.max(tops[tile], axis=0, keepdims=True)
            out[tile : tile + 1, :] = top
            out[tiles + tile : tiles + tile + 1, :] = jnp.sum(
                sums[tile] * jnp.exp2(tops[tile] - top), axis=0, keepdims=True
            )
        half = tiles // 2
        out[2 * tiles : 2 * tiles + half, :] = delta[...]


def grad_body(scale, inv_root, owners, backs, slots, carried, last, info, starts, rows, mine, other, *refs):
    refs = list(refs)
    keys = [refs.pop(0) for _ in backs]
    values = [refs.pop(0) for _ in backs]
    stores = [refs.pop(0).at[slot] if back else None for back, slot in zip(backs, slots)]
    query_in = refs.pop(0) if carried else None
    kept = refs.pop(0)
    sends = [refs.pop(0) for _ in range(owners - 1)]
    query_parts = [refs.pop(0) for _ in range(2)] if last else None
    query_out, logs, deltas, key_acc, value_acc = refs
    ctx, head = info[0], info[1]
    tiles, width = rows.shape[1], rows.shape[2]
    shard_rows, size = key_acc.shape
    half = tiles // 2
    query_out[...] = query_in[...] if carried else jnp.zeros(query_out.shape, jnp.float32)
    for tile in range(tiles):
        twin = (tile + half) % tiles
        top_a, top_b = mine[tile : tile + 1, :], other[twin : twin + 1, :]
        sum_a, sum_b = mine[tiles + tile : tiles + tile + 1, :], other[tiles + twin : tiles + twin + 1, :]
        top = jnp.maximum(top_a, top_b)
        total = sum_a * jnp.exp2(top_a - top) + sum_b * jnp.exp2(top_b - top)
        logs[tile] = top + jnp.log2(total)
        source = mine if tile < half else other
        at = 2 * tiles + tile % half
        deltas[tile] = source[at : at + 1, :]
    part = shard_rows // owners
    for slot, back in enumerate(backs):
        key_ref, value_ref, store = keys[slot], values[slot], stores[slot]
        key_acc[...] = jnp.zeros(key_acc.shape, jnp.float32)
        value_acc[...] = jnp.zeros(value_acc.shape, jnp.float32)

        def visit(query_tile, base, count, edge, key_ref=key_ref, value_ref=value_ref, store=store):
            query, grad = rows[0, query_tile], rows[1, query_tile]
            log_total, delta = logs[query_tile], deltas[query_tile]
            score_grads = []
            for offset in range(0, count, TILE):
                at = pl.ds(base + offset, TILE)
                prob_grad = lax.dot_general(value_ref[at, :], grad, NT, preferred_element_type=jnp.float32)
                if store is None:
                    score = lax.dot_general(key_ref[at, :], query, NT, preferred_element_type=jnp.float32) * scale
                    if edge is not None:
                        score = jnp.where(tile_mask(edge, offset, TILE, width), score, masked_score)
                else:
                    score = store[query_tile, at, :]
                prob = jnp.exp2(score - log_total)
                score_grad = (prob * (prob_grad - delta)).astype(jnp.bfloat16)
                value_acc[at, :] += jnp.dot(prob.astype(jnp.bfloat16), grad, preferred_element_type=jnp.float32)
                key_acc[at, :] += jnp.dot(score_grad, query, preferred_element_type=jnp.float32)
                score_grads.append(score_grad)
            score_grad = jnp.concatenate(score_grads, axis=0)
            query_out[query_tile] += lax.dot_general(
                key_ref[pl.ds(base, count), :],
                score_grad,
                (((0,), (0,)), ((), ())),
                preferred_element_type=jnp.float32,
            )

        each_tile(ctx, starts, back, shard_rows, tiles, visit)

        for turn in range(owners):
            at = pl.ds(pl.multiple_of(lax.rem(head + turn, owners) * part, part), part)
            out = sends[turn - 1] if turn else kept
            out[slot, :, :size] = (key_acc[at, :] * inv_root).astype(out.dtype)
            out[slot, :, size:] = value_acc[at, :].astype(out.dtype)
    if last:
        query_parts[0][...] = query_out[:half]
        query_parts[1][...] = query_out[half:]


def vmem(count):
    return [pl.BlockSpec(memory_space=pltpu.VMEM)] * count


def smem(count):
    return [pl.BlockSpec(memory_space=pltpu.SMEM)] * count


def limit(mib):
    return pltpu.CompilerParams(vmem_limit_bytes=mib << 20)


def local(queries, keys, values, output, output_grad, block_doc):
    shard_rows, heads, size = queries.shape
    cycle = lax.axis_size("ctx")
    owners = lax.axis_size("head")
    steps = cycle // 2
    ctx = lax.axis_index("ctx").astype(jnp.int32)
    head = lax.axis_index("head").astype(jnp.int32)
    inv_root = size ** (-0.5)
    scale = inv_root * math.log2(math.e)
    half = shard_rows // TILE
    tiles, width = 2 * half, heads * TILE
    part = shard_rows // owners
    twins = [(i, i ^ 1) for i in range(cycle)]

    def swap(array):
        return lax.ppermute(array, "ctx", twins)

    def shift(array, back):
        return lax.ppermute(array, "ctx", [(i, i + 2 * back) for i in range(cycle - 2 * back)])

    def unshift(array, back):
        return lax.ppermute(array, "ctx", [(i + 2 * back, i) for i in range(cycle - 2 * back)])

    def turned(array, turn):
        return lax.ppermute(array, "head", [(i, (i + turn) % owners) for i in range(owners)])

    key_parts = [keys]
    for back in range(1, steps):
        key_parts.append(shift(keys, back))

    def tiled(array):
        return array.reshape(half, TILE, heads, size).transpose(0, 2, 1, 3).reshape(half, width, size)

    own_rows = jnp.stack([tiled(queries), tiled(output_grad)])
    other_rows = swap(own_rows)
    rows = jnp.concatenate([own_rows, other_rows], axis=1)
    value_parts = [values]
    for back in range(1, steps):
        value_parts.append(shift(values, back))
    delta = jnp.sum(output_grad.astype(jnp.float32) * output.astype(jnp.float32), axis=-1)
    delta = delta.reshape(half, TILE, heads).transpose(0, 2, 1).reshape(half, width)
    starts = BLK * jnp.sum((block_doc[None, :] < block_doc[:, None]).astype(jnp.int32), axis=1)
    info = jnp.stack([ctx, head])

    def stored(count):
        return jax.ShapeDtypeStruct((count, tiles, shard_rows, width), jnp.float32)

    running = (jax.ShapeDtypeStruct((tiles, 8, width), jnp.float32),) * 2
    tops, sums = pl.pallas_call(
        lambda *refs: near_stats_body(scale, *refs),
        out_shape=running,
        in_specs=smem(2) + vmem(2),
        out_specs=tuple(vmem(2)),
        compiler_params=limit(12),
        name="near_stats",
    )(info, starts, rows, keys)

    def far_stats(backs, tops, sums, last):
        return pl.pallas_call(
            lambda *refs: far_stats_body(scale, backs, last, *refs),
            out_shape=(stored(len(backs)),)
            + ((jax.ShapeDtypeStruct((4 * tiles, width), jnp.float32),) if last else ())
            + running,
            in_specs=smem(2) + vmem(4 + len(backs)),
            out_specs=tuple(vmem(4 if last else 3)),
            compiler_params=limit(12),
        )(info, starts, rows, delta, tops, sums, *[key_parts[back] for back in backs])

    store_1, tops, sums = far_stats((1,), tops, sums, False)
    store_23, stats = far_stats((2, 3), tops, sums, True)[:2]
    stores = [(None, 0), (store_1, 0), (store_23, 0), (store_23, 1)]
    other = swap(stats)

    def grads(backs, query_in, last):
        carried = query_in is not None
        count = len(backs)
        ins = [key_parts[back] for back in backs] + [value_parts[back] for back in backs]
        ins = ins + [stores[back][0] for back in backs if back] + ([query_in] if carried else [])
        slots = [stores[back][1] for back in backs]
        whole_query = jax.ShapeDtypeStruct((tiles, size, width), jnp.float32)
        half_query = jax.ShapeDtypeStruct((half, size, width), jnp.float32)
        outs = (jax.ShapeDtypeStruct((count, part, 2 * size), jnp.float32),)
        outs = outs + (jax.ShapeDtypeStruct((count, part, 2 * size), jnp.bfloat16),) * (owners - 1)
        outs = outs + ((half_query,) * 2 if last else ()) + (whole_query,)
        return pl.pallas_call(
            lambda *refs: grad_body(scale, inv_root, owners, backs, slots, carried, last, *refs),
            out_shape=outs,
            in_specs=smem(2) + vmem(3 + len(ins)),
            out_specs=tuple(vmem(len(outs))),
            scratch_shapes=[pltpu.VMEM((tiles, 1, width), jnp.float32)] * 2
            + [pltpu.VMEM((shard_rows, size), jnp.float32)] * 2,
            input_output_aliases={4 + len(ins): len(outs) - 1} if carried else {},
            compiler_params=limit(16),
        )(info, starts, rows, stats, other, *ins)

    kept_0, *sends_0, query_acc = grads((0,), None, False)
    kept_a, *sends_a, query_acc = grads((3, 2), query_acc, False)
    kept_b, *sends_b, query_own, query_other, _ = grads((1,), query_acc, True)
    came_a, came_b = [], []
    for turn in range(1, owners):
        both = jnp.concatenate([sends_a[turn - 1], sends_0[turn - 1]], axis=0)
        came_a.append(turned(both, turn))
        came_b.append(turned(sends_b[turn - 1], turn))
    query_came = swap(query_other)
    query_sum = query_own + query_came
    query_grad = (query_sum * inv_root).reshape(half, size, heads, TILE).transpose(0, 3, 2, 1)
    query_grad = query_grad.reshape(shard_rows, heads, size).astype(jnp.bfloat16)

    total_a = kept_a + sum(came[:2].astype(jnp.float32) for came in came_a)
    low_3, low_2 = total_a[0].astype(jnp.bfloat16), total_a[1].astype(jnp.bfloat16)
    total = kept_0[0] + sum(came[2].astype(jnp.float32) for came in came_a)
    low_1 = (kept_b[0] + sum(came[0].astype(jnp.float32) for came in came_b)).astype(jnp.bfloat16)
    back_3 = unshift(low_3, 3)
    back_2 = unshift(low_2, 2)
    back_1 = unshift(low_1, 1)
    total, query_grad = lax.optimization_barrier((total, query_grad))
    total = total + back_3.astype(jnp.float32) + back_2.astype(jnp.float32) + back_1.astype(jnp.float32)
    total = total.astype(jnp.bfloat16)
    return query_grad, total[:, :size], total[:, size:]


def solution(mesh):
    placed = (
        P(("dp", "ctx"), "head", None),
        P(("dp", "ctx"), None),
        P(("dp", "ctx"), None),
        P(("dp", "ctx"), "head", None),
        P(("dp", "ctx"), "head", None),
        P("dp"),
    )
    return jax.shard_map(
        local,
        mesh=mesh,
        in_specs=placed,
        out_specs=(
            P(("dp", "ctx"), "head", None),
            P(("dp", "ctx", "head"), None),
            P(("dp", "ctx", "head"), None),
        ),
        check_vma=False,
    )
```

```python
import math

import jax
import jax.numpy as jnp
from jax import lax
from jax.experimental import pallas as pl
from jax.experimental.pallas import tpu as pltpu
from jax.sharding import PartitionSpec as P


BLK = 128
TILE = 256
floor_score = -1.0e30
masked_score = -2.0e30

NT = (((1,), (1,)), ((), ()))


def tile_bounds(ctx, starts, back, key_tile, key_rows, query_tile, shard_rows):
    key_base = (ctx - 2 * back) * shard_rows + key_tile * key_rows
    partner = ctx + 1 - 2 * lax.rem(ctx, 2)
    shard = jnp.where(query_tile < 2, ctx, partner)
    query_base = shard * shard_rows + lax.rem(query_tile, 2) * TILE
    block = lax.div(query_base, BLK)
    first, last = starts[block], starts[block + 1]
    seen = (key_base <= query_base + TILE - 1) & (key_base + key_rows - 1 >= first)
    inside = (key_base + key_rows - 1 <= query_base) & (key_base >= last)
    return (key_base, query_base, first, last), seen, inside


def tile_mask(edge, offset, rows, width):
    key_base, query_base, first, last = edge
    key_pos = key_base + offset + lax.broadcasted_iota(jnp.int32, (rows, width), 0)
    lane = lax.rem(lax.broadcasted_iota(jnp.int32, (1, width), 1), TILE)
    query_pos = query_base + lane
    start = jnp.where(lane < BLK, first, last)
    return (key_pos <= query_pos) & (key_pos >= start)


def each_tile(ctx, starts, back, shard_rows, first, last, visit):
    def step(query_tile, carry):
        _, seen, inside = tile_bounds(ctx, starts, back, 0, shard_rows, query_tile, shard_rows)

        @pl.when(inside)
        def _():
            visit(query_tile, 0, shard_rows, None)

        @pl.when(seen & jnp.logical_not(inside))
        def _():
            def part(key_tile, carry):
                edge, seen, _ = tile_bounds(ctx, starts, back, key_tile, TILE, query_tile, shard_rows)

                @pl.when(seen)
                def _():
                    visit(query_tile, pl.multiple_of(key_tile * TILE, TILE), TILE, edge)

                return carry

            lax.fori_loop(0, shard_rows // TILE, part, 0)

        return carry

    @pl.when(ctx >= 2 * back)
    def _():
        lax.fori_loop(first, last, step, 0)


def stat_chunk(scale, ctx, starts, back, rows, key_ref, store, tops, sums):
    tiles, width = rows.shape[1], rows.shape[2]
    sub = 32

    def visit(query_tile, base, count, edge, keep=True):
        top = tops[query_tile]
        total = sums[query_tile]
        scores = lax.dot_general(
            key_ref[pl.ds(base, count), :], rows[0, query_tile], NT, preferred_element_type=jnp.float32
        )
        for offset in range(0, count, sub):
            score = scores[offset : offset + sub] * scale
            if edge is not None:
                score = jnp.where(tile_mask(edge, offset, sub, width), score, masked_score)
            if keep:
                store[query_tile, pl.ds(base + offset, sub), :] = score
            score = score.reshape(sub // 8, 8, width)
            new = jnp.maximum(top, jnp.max(score, axis=0))
            total = total * jnp.exp2(top - new) + jnp.sum(jnp.exp2(score - new[None]), axis=0)
            top = new
        sums[query_tile] = total
        tops[query_tile] = top

    kept = store.shape[0]
    each_tile(ctx, starts, back, key_ref.shape[0], 0, kept, visit)
    if kept < tiles:
        each_tile(ctx, starts, back, key_ref.shape[0], kept, tiles, lambda *args: visit(*args, keep=False))


def near_stats_body(scale, info, docs, rows, delta, key_ref, starts, store, delta_out, tops, sums):
    start = jnp.int32(0)
    starts[0] = start
    for block in range(1, docs.shape[0]):
        start = jnp.where(docs[block] == docs[block - 1], start, block * BLK)
        starts[block] = start
    delta_out[...] = delta[...]
    tops[...] = jnp.full(tops.shape, floor_score, jnp.float32)
    sums[...] = jnp.zeros(sums.shape, jnp.float32)
    stat_chunk(scale, info[0], starts, 0, rows, key_ref, store.at[0], tops, sums)


def far_stats_body(scale, backs, last, info, starts, rows, delta, tops_in, sums_in, *refs):
    count = len(backs)
    keys, store, outs = refs[:count], refs[count], refs[count + 1 :]
    tiles = rows.shape[1]
    tops, sums = outs[-2:]
    tops[...] = tops_in[...]
    sums[...] = sums_in[...]
    for slot, (back, key_ref) in enumerate(zip(backs, keys)):
        stat_chunk(scale, info[0], starts, back, rows, key_ref, store.at[slot], tops, sums)
    if last:
        out = outs[0]
        for tile in range(tiles):
            top = jnp.max(tops[tile], axis=0, keepdims=True)
            out[tile : tile + 1, :] = top
            out[tiles + tile : tiles + tile + 1, :] = jnp.sum(
                sums[tile] * jnp.exp2(tops[tile] - top), axis=0, keepdims=True
            )
        half = tiles // 2
        out[2 * tiles : 2 * tiles + half, :] = delta[...]


def grad_body(scale, inv_root, owners, backs, slots, carried, last, info, starts, rows, mine, other, *refs):
    refs = list(refs)
    keys = [refs.pop(0) for _ in backs]
    values = [refs.pop(0) for _ in backs]
    stores = [refs.pop(0).at[slot] for slot in slots]
    query_in = refs.pop(0) if carried else None
    kept = refs.pop(0)
    sends = [refs.pop(0) for _ in range(owners - 1)]
    query_parts = [refs.pop(0) for _ in range(2)] if last else None
    query_out, logs, deltas, key_acc, value_acc = refs
    ctx, head = info[0], info[1]
    tiles, width = rows.shape[1], rows.shape[2]
    shard_rows, size = key_acc.shape
    half = tiles // 2
    query_out[...] = query_in[...] if carried else jnp.zeros(query_out.shape, jnp.float32)
    for tile in range(tiles):
        twin = (tile + half) % tiles
        top_a, top_b = mine[tile : tile + 1, :], other[twin : twin + 1, :]
        sum_a, sum_b = mine[tiles + tile : tiles + tile + 1, :], other[tiles + twin : tiles + twin + 1, :]
        top = jnp.maximum(top_a, top_b)
        total = sum_a * jnp.exp2(top_a - top) + sum_b * jnp.exp2(top_b - top)
        logs[tile] = top + jnp.log2(total)
        source = mine if tile < half else other
        at = 2 * tiles + tile % half
        deltas[tile] = source[at : at + 1, :]
    part = shard_rows // owners
    for slot, back in enumerate(backs):
        key_ref, value_ref, store = keys[slot], values[slot], stores[slot]
        key_acc[...] = jnp.zeros(key_acc.shape, jnp.float32)
        value_acc[...] = jnp.zeros(value_acc.shape, jnp.float32)

        def visit(query_tile, base, count, edge, keep=True, key_ref=key_ref, value_ref=value_ref, store=store):
            query, grad = rows[0, query_tile], rows[1, query_tile]
            log_total, delta = logs[query_tile], deltas[query_tile]
            score_grads = []
            for offset in range(0, count, TILE):
                at = pl.ds(base + offset, TILE)
                prob_grad = lax.dot_general(value_ref[at, :], grad, NT, preferred_element_type=jnp.float32)
                if not keep:
                    score = lax.dot_general(key_ref[at, :], query, NT, preferred_element_type=jnp.float32) * scale
                    if edge is not None:
                        score = jnp.where(tile_mask(edge, offset, TILE, width), score, masked_score)
                else:
                    score = store[query_tile, at, :]
                prob = jnp.exp2(score - log_total)
                score_grad = (prob * (prob_grad - delta)).astype(jnp.bfloat16)
                value_acc[at, :] += jnp.dot(prob.astype(jnp.bfloat16), grad, preferred_element_type=jnp.float32)
                key_acc[at, :] += jnp.dot(score_grad, query, preferred_element_type=jnp.float32)
                score_grads.append(score_grad)
            score_grad = jnp.concatenate(score_grads, axis=0)
            query_out[query_tile] += lax.dot_general(
                key_ref[pl.ds(base, count), :],
                score_grad,
                (((0,), (0,)), ((), ())),
                preferred_element_type=jnp.float32,
            )

        stored = store.shape[0]
        each_tile(ctx, starts, back, shard_rows, 0, stored, visit)
        if stored < tiles:
            each_tile(ctx, starts, back, shard_rows, stored, tiles, lambda *args, visit=visit: visit(*args, keep=False))

        for turn in range(owners):
            at = pl.ds(pl.multiple_of(lax.rem(head + turn, owners) * part, part), part)
            out = sends[turn - 1] if turn else kept
            out[slot, :, :size] = (key_acc[at, :] * inv_root).astype(out.dtype)
            out[slot, :, size:] = value_acc[at, :].astype(out.dtype)
    if last:
        query_parts[0][...] = query_out[:half]
        query_parts[1][...] = query_out[half:]


def vmem(count):
    return [pl.BlockSpec(memory_space=pltpu.VMEM)] * count


def smem(count):
    return [pl.BlockSpec(memory_space=pltpu.SMEM)] * count


def limit(mib):
    return pltpu.CompilerParams(vmem_limit_bytes=mib << 20)


def local(queries, keys, values, output, output_grad, block_doc):
    shard_rows, heads, size = queries.shape
    cycle = lax.axis_size("ctx")
    owners = lax.axis_size("head")
    steps = cycle // 2
    ctx = lax.axis_index("ctx").astype(jnp.int32)
    head = lax.axis_index("head").astype(jnp.int32)
    inv_root = size ** (-0.5)
    scale = inv_root * math.log2(math.e)
    half = shard_rows // TILE
    tiles, width = 2 * half, heads * TILE
    part = shard_rows // owners
    twins = [(i, i ^ 1) for i in range(cycle)]

    def swap(array):
        return lax.ppermute(array, "ctx", twins)

    def shift(array, back):
        return lax.ppermute(array, "ctx", [(i, i + 2 * back) for i in range(cycle - 2 * back)])

    def unshift(array, back):
        return lax.ppermute(array, "ctx", [(i + 2 * back, i) for i in range(cycle - 2 * back)])

    def turned(array, turn):
        return lax.ppermute(array, "head", [(i, (i + turn) % owners) for i in range(owners)])

    key_parts = [keys]
    for back in range(1, steps):
        key_parts.append(shift(keys, back))

    def tiled(array):
        return array.reshape(half, TILE, heads, size).transpose(0, 2, 1, 3).reshape(half, width, size)

    own_rows = jnp.stack([tiled(queries), tiled(output_grad)])
    other_rows = swap(own_rows)
    rows = jnp.concatenate([own_rows, other_rows], axis=1)
    value_parts = [values]
    for back in range(1, steps):
        value_parts.append(shift(values, back))
    delta = jnp.sum(output_grad.astype(jnp.float32) * output.astype(jnp.float32), axis=-1)
    delta = delta.reshape(half, TILE, heads).transpose(0, 2, 1).reshape(half, width)
    info = jnp.stack([ctx, head])

    def stored(count, kept=tiles):
        return jax.ShapeDtypeStruct((count, kept, shard_rows, width), jnp.float32)

    running = (jax.ShapeDtypeStruct((tiles, 8, width), jnp.float32),) * 2
    starts, store_0, delta, tops, sums = pl.pallas_call(
        lambda *refs: near_stats_body(scale, *refs),
        out_shape=(jax.ShapeDtypeStruct(block_doc.shape, jnp.int32), stored(1), jax.ShapeDtypeStruct(delta.shape, jnp.float32)) + running,
        in_specs=smem(2) + vmem(3),
        out_specs=tuple(smem(1) + vmem(4)),
        compiler_params=limit(12),
        name="near_stats",
    )(info, block_doc, rows, delta, keys)

    def far_stats(backs, tops, sums, last):
        return pl.pallas_call(
            lambda *refs: far_stats_body(scale, backs, last, *refs),
            out_shape=(stored(len(backs)),)
            + ((jax.ShapeDtypeStruct((4 * tiles, width), jnp.float32),) if last else ())
            + running,
            in_specs=smem(2) + vmem(4 + len(backs)),
            out_specs=tuple(vmem(4 if last else 3)),
            compiler_params=limit(12),
        )(info, starts, rows, delta, tops, sums, *[key_parts[back] for back in backs])

    store_1, tops, sums = far_stats((1,), tops, sums, False)
    store_23, stats = far_stats((2, 3), tops, sums, True)[:2]
    stores = [(store_0, 0), (store_1, 0), (store_23, 0), (store_23, 1)]
    other = swap(stats)

    def grads(backs, query_in, last):
        carried = query_in is not None
        count = len(backs)
        ins = [key_parts[back] for back in backs] + [value_parts[back] for back in backs]
        ins = ins + [stores[back][0] for back in backs] + ([query_in] if carried else [])
        slots = [stores[back][1] for back in backs]
        whole_query = jax.ShapeDtypeStruct((tiles, size, width), jnp.float32)
        half_query = jax.ShapeDtypeStruct((half, size, width), jnp.float32)
        outs = (jax.ShapeDtypeStruct((count, part, 2 * size), jnp.float32),)
        outs = outs + (jax.ShapeDtypeStruct((count, part, 2 * size), jnp.bfloat16),) * (owners - 1)
        outs = outs + ((half_query,) * 2 if last else ()) + (whole_query,)
        return pl.pallas_call(
            lambda *refs: grad_body(scale, inv_root, owners, backs, slots, carried, last, *refs),
            out_shape=outs,
            in_specs=smem(2) + vmem(3 + len(ins)),
            out_specs=tuple(vmem(len(outs))),
            scratch_shapes=[pltpu.VMEM((tiles, 1, width), jnp.float32)] * 2
            + [pltpu.VMEM((shard_rows, size), jnp.float32)] * 2,
            input_output_aliases={4 + len(ins): len(outs) - 1} if carried else {},
            compiler_params=limit(16),
        )(info, starts, rows, stats, other, *ins)

    kept_0, *sends_0, query_acc = grads((0,), None, False)
    kept_a, *sends_a, query_acc = grads((3, 2), query_acc, False)
    kept_b, *sends_b, query_own, query_other, _ = grads((1,), query_acc, True)
    came_a, came_b = [], []
    for turn in range(1, owners):
        both = jnp.concatenate([sends_a[turn - 1], sends_0[turn - 1]], axis=0)
        came_a.append(turned(both, turn))
        came_b.append(turned(sends_b[turn - 1], turn))
    query_came = swap(query_other)
    query_sum = query_own + query_came
    query_grad = (query_sum * inv_root).reshape(half, size, heads, TILE).transpose(0, 3, 2, 1)
    query_grad = query_grad.reshape(shard_rows, heads, size).astype(jnp.bfloat16)

    total_a = kept_a + sum(came[:2].astype(jnp.float32) for came in came_a)
    low_3, low_2 = total_a[0].astype(jnp.bfloat16), total_a[1].astype(jnp.bfloat16)
    total = kept_0[0] + sum(came[2].astype(jnp.float32) for came in came_a)
    low_1 = (kept_b[0] + sum(came[0].astype(jnp.float32) for came in came_b)).astype(jnp.bfloat16)
    back_3 = unshift(low_3, 3)
    back_2 = unshift(low_2, 2)
    back_1 = unshift(low_1, 1)
    total, query_grad = lax.optimization_barrier((total, query_grad))
    total = total + back_3.astype(jnp.float32) + back_2.astype(jnp.float32) + back_1.astype(jnp.float32)
    total = total.astype(jnp.bfloat16)
    return query_grad, total[:, :size], total[:, size:]


def solution(mesh):
    placed = (
        P(("dp", "ctx"), "head", None),
        P(("dp", "ctx"), None),
        P(("dp", "ctx"), None),
        P(("dp", "ctx"), "head", None),
        P(("dp", "ctx"), "head", None),
        P("dp"),
    )
    return jax.shard_map(
        local,
        mesh=mesh,
        in_specs=placed,
        out_specs=(
            P(("dp", "ctx"), "head", None),
            P(("dp", "ctx", "head"), None),
            P(("dp", "ctx", "head"), None),
        ),
        check_vma=False,
    )
```
